32 devices in a mesh: seq: 8 (over z, x), head: 4 (over y, core).
Axes of the slice: x: 2, y: 2, z: 4, core: 2. Of those that a mesh axis runs over, the one named last changes fastest.
Arguments:
- queries: bfloat16 [3072, 1536], P('seq', 'head'), may hold values from -6 to 6
- key_vectors: bfloat16 [3072, 1536], P('seq', 'head'), may hold values from -6 to 6
- value_vectors: bfloat16 [3072, 1536], P('seq', 'head'), may hold values from -6 to 6
- out_weight: bfloat16 [1536, 5120], P('head'), may hold values from -0.15625 to 0.15625
- d_output: bfloat16 [3072, 5120], P('seq', 'head'), may hold values from -6 to 6
- block_keys: int32 [24, 24], replicated, may hold values from 0 to 23, as said below
- key_count: int32 [24], replicated, may hold values from 12 to 24
- frame_slot: int32 [8], replicated, may hold values from 0 to 7, each once
Outputs:
- layer_out: bfloat16 [3072, 5120], P('seq', 'head')
- d_query: bfloat16 [3072, 1536], P('seq', 'head')
- d_key: bfloat16 [3072, 1536], P('seq', 'head')
- d_value: bfloat16 [3072, 1536], P('seq', 'head')
- d_weight: bfloat16 [1536, 5120], P('head', 'seq')
The draws below stay inside these ranges and needn't reach their ends.
Inputs may be any that keep to these rules, and one draw needn't show every extreme that they name: `block_keys`: row l names distinct logical key blocks for the logical query block l; the first 3 entries are the blocks of the query's own frame, the query block itself first; only the first key_count[l] entries are attended.
All inputs are finite; a program needn't handle non-finite values.
Results may differ from the reference program's by a relative error of at most 0.018.
Values may be sent and summed in bfloat16 or wider, within the bound.
A program may use at most 192 MiB of HBM per device.

```python
import math
import jax
import jax.numpy as jnp
from jax import lax

D = 5120
HD = 128
HEAD_DEV = 3
BLOCK = 128
FRAME_TOK = 384
NKB = 24
T_DEV = 384
FRAMES = 8
TOKENS = 3072
HEADS = 12
N_SEQ = 8
N_HEAD = 4


def drawn_pair(key):
    base_key = jax.random.fold_in(key, 41)
    shape = (TOKENS, HEADS * HD)
    query_draw = jnp.clip(jax.random.normal(jax.random.fold_in(base_key, 1), shape, jnp.float32), -6.0, 6.0)
    key_draw = jnp.clip(jax.random.normal(jax.random.fold_in(base_key, 2), shape, jnp.float32), -6.0, 6.0)
    return (query_draw, key_draw)


def draw_queries(key, part):
    return drawn_pair(key)[0].astype(jnp.bfloat16)


def draw_key_vectors(key, part):
    return drawn_pair(key)[1].astype(jnp.bfloat16)


def radial_lists(key):
    base_key = jax.random.fold_in(key, 23)
    block_count = TOKENS // BLOCK
    per_frame = FRAME_TOK // BLOCK
    block_ids = jnp.arange(block_count, dtype=jnp.int32)
    distance = jnp.abs((block_ids // per_frame)[:, None] - (block_ids // per_frame)[None, :])
    noise = jax.random.randint(jax.random.fold_in(base_key, 1), (block_count, block_count), 0, 4096)
    priority = noise // (1 + distance * distance)
    tiebreak = block_count - 1 - block_ids[None, :]
    ranking = priority * block_count + tiebreak
    ranking = jnp.where(distance == 0, (1 << 22) + tiebreak, ranking)
    ranking = jnp.where(block_ids[:, None] == block_ids[None, :], 1 << 23, ranking)
    ignored, chosen = lax.top_k(ranking, NKB)
    counts = jax.random.randint(jax.random.fold_in(base_key, 2), (block_count,), NKB // 2, NKB + 1)
    fullest = jax.random.randint(jax.random.fold_in(base_key, 3), (), 0, block_count)
    counts = jnp.where(block_ids == fullest, NKB, counts)
    return (chosen.astype(jnp.int32), counts.astype(jnp.int32))


def draw_block_keys(key, part):
    return radial_lists(key)[0]


def draw_key_count(key, part):
    return radial_lists(key)[1]


def strengthened(array, key, source, target, blocks, factor):
    owner, partner = [(jnp.arange(array.shape[position]) // (array.shape[position] // blocks)).reshape([-1 if axis == position else 1 for axis in range(array.ndim)]) for position in (source, target)]
    chosen = jax.random.permutation(key, blocks)[partner]
    strong = (owner == chosen) | (owner == (partner + blocks // 2) % blocks)
    return jnp.where(strong, factor * array, array)


def shard_levels(key, extent, cuts, least, largest):
    level = 1.0
    for dim, parts in cuts:
        heights = jax.random.uniform(jax.random.fold_in(jax.random.fold_in(key, 6), dim), (parts,), jnp.float32, least / len(cuts), largest / len(cuts))
        level = level * jnp.repeat(jnp.exp(heights), extent[dim] // parts).reshape((-1,) + (1,) * (len(extent) - 1 - dim))
    return level


def gaussian(stream_key, extent, scale, limit, pieces=(), kind=jnp.bfloat16):
    level = shard_levels(stream_key, extent, pieces, -0.22, 0.18) if pieces else 1.0
    values = jax.random.normal(stream_key, extent, jnp.float32) * scale * level
    return jnp.minimum(jnp.maximum(values, -limit), limit).astype(kind)


def gaussian_with(rng, shape, scale, most, shards, heavy, kind=jnp.bfloat16):
    values = scale * jax.random.normal(rng, shape, jnp.float32)
    if shards:
        values = values * shard_levels(rng, shape, shards, -0.22, 0.18)
    return jnp.clip(strengthened(values, jax.random.fold_in(rng, 3), *heavy), -most, most).astype(kind)


def setup_inputs(seed: int = 0) -> dict:
    streams_of = jax.random.split(jax.random.key(seed), 9)
    queries = draw_queries(jax.random.fold_in(streams_of[8], 71), 0)
    key_vectors = draw_key_vectors(jax.random.fold_in(streams_of[8], 71), 0)
    value_vectors = gaussian(streams_of[2], (TOKENS, HEADS * HD), 1.0, 6.0, ((0, 8), (1, 4)))
    out_weight = gaussian(streams_of[3], (HEADS * HD, D), (HEADS * HD) ** -0.5, 0.15625, ((0, 4),))
    d_output = gaussian_with(streams_of[4], (TOKENS, D), 1.0, 6.0, ((0, 8), (1, 4)), (0, 1, 8, 2.0))
    block_keys = draw_block_keys(jax.random.fold_in(streams_of[8], 71), 0)
    key_count = draw_key_count(jax.random.fold_in(streams_of[8], 71), 0)
    frame_slot = jax.random.permutation(streams_of[7], FRAMES).astype(jnp.int32)
    return dict(queries=queries, key_vectors=key_vectors, value_vectors=value_vectors, out_weight=out_weight, d_output=d_output, block_keys=block_keys, key_count=key_count, frame_slot=frame_slot)


def rounded(values):
    return lax.optimization_barrier(values.astype(jnp.bfloat16)).astype(jnp.float32)

def storage_lists(block_keys, key_count, frame_slot):
    per_frame = FRAME_TOK // BLOCK
    frames = frame_slot.shape[0]
    block_count = block_keys.shape[0]
    frame_at = jnp.zeros((frames,), jnp.int32).at[frame_slot].set(jnp.arange(frames, dtype=jnp.int32))
    block_ids = jnp.arange(block_count, dtype=jnp.int32)
    logical = frame_at[block_ids // per_frame] * per_frame + block_ids % per_frame
    entries = block_keys[logical]
    counts = key_count[logical]
    stored = frame_slot[entries // per_frame] * per_frame + entries % per_frame
    return (stored.astype(jnp.int32), counts.astype(jnp.int32))

def reference(queries, key_vectors, value_vectors, out_weight, d_output, block_keys, key_count, frame_slot):
    col_count = queries.shape[1]
    head_count = col_count // HD
    block_count = block_keys.shape[0]
    score_scale = 1.0 / math.sqrt(HD)
    stored, counts = storage_lists(block_keys, key_count, frame_slot)
    d_attn = jnp.dot(d_output, out_weight.T, preferred_element_type=jnp.float32).astype(jnp.bfloat16)
    key_blocks = key_vectors.reshape(block_count, BLOCK, head_count, HD)
    value_blocks = value_vectors.reshape(block_count, BLOCK, head_count, HD)
    per_group = T_DEV // BLOCK
    key_span = NKB * BLOCK

    def one_group(carried, inputs):
        key_accum, value_accum = carried
        group_query, group_grad, group_lists, group_counts = inputs
        selected_keys = key_blocks[group_lists].reshape(per_group, key_span, head_count, HD).astype(jnp.float32)
        selected_values = value_blocks[group_lists].reshape(per_group, key_span, head_count, HD).astype(jnp.float32)
        valid_keys = jnp.repeat(jnp.arange(NKB)[None, :] < group_counts[:, None], BLOCK, axis=1)
        query_full = group_query.astype(jnp.float32)
        scores = jnp.einsum('bqhd,bkhd->bhqk', query_full, selected_keys) * score_scale
        scores = jnp.where(valid_keys[:, None, None, :], scores, -1e+30)
        row_peak = lax.optimization_barrier(jnp.max(scores, axis=-1, keepdims=True))
        exp_scores = jnp.exp(scores - row_peak)
        attn_weights = exp_scores / lax.optimization_barrier(jnp.sum(exp_scores, axis=-1, keepdims=True))
        reduced_precision_weights = rounded(attn_weights)
        attn_out = rounded(jnp.einsum('bhqk,bkhd->bqhd', reduced_precision_weights, selected_values))
        grad_full = group_grad.astype(jnp.float32)
        row_delta = lax.optimization_barrier(jnp.sum(grad_full * attn_out, axis=-1))
        grad_weights = jnp.einsum('bqhd,bkhd->bhqk', grad_full, selected_values)
        score_gradient = rounded(attn_weights * (grad_weights - jnp.transpose(row_delta, (0, 2, 1))[..., None]))
        grad_query = rounded(jnp.einsum('bhqk,bkhd->bqhd', score_gradient, selected_keys) * score_scale)
        key_part = jnp.einsum('bhqk,bqhd->bkhd', score_gradient, query_full).reshape(per_group * NKB, BLOCK, col_count)
        value_part = jnp.einsum('bhqk,bqhd->bkhd', reduced_precision_weights, grad_full).reshape(per_group * NKB, BLOCK, col_count)
        flat_lists = group_lists.reshape(-1)
        key_accum = key_accum.at[flat_lists].add(key_part)
        value_accum = value_accum.at[flat_lists].add(value_part)
        return ((key_accum, value_accum), (attn_out, grad_query))
    inputs = (queries.reshape(N_SEQ, per_group, BLOCK, head_count, HD), d_attn.reshape(N_SEQ, per_group, BLOCK, head_count, HD), stored.reshape(N_SEQ, per_group, NKB), counts.reshape(N_SEQ, per_group))
    initial = (jnp.zeros((block_count, BLOCK, col_count), jnp.float32), jnp.zeros((block_count, BLOCK, col_count), jnp.float32))
    (key_accum, value_accum), (attn_all, grad_all) = lax.scan(one_group, initial, inputs)
    attn_low = attn_all.reshape(TOKENS, col_count).astype(jnp.bfloat16)
    d_query = grad_all.reshape(TOKENS, col_count).astype(jnp.bfloat16)
    d_key = (key_accum.reshape(TOKENS, col_count) * score_scale).astype(jnp.bfloat16)
    d_value = value_accum.reshape(TOKENS, col_count).astype(jnp.bfloat16)
    group_cols = HEAD_DEV * HD
    layer_sum = jnp.zeros((TOKENS, D), jnp.float32)
    for head_group in range(N_HEAD):
        col_start = head_group * group_cols
        partial_value = jnp.dot(attn_low[:, col_start:col_start + group_cols], out_weight[col_start:col_start + group_cols], preferred_element_type=jnp.float32)
        layer_sum = layer_sum + rounded(partial_value)
    layer_out = layer_sum.astype(jnp.bfloat16)
    weight_sum = jnp.zeros((col_count, D), jnp.float32)
    for seq_group in range(N_SEQ):
        row_start = seq_group * T_DEV
        partial_value = jnp.dot(attn_low[row_start:row_start + T_DEV].T, d_output[row_start:row_start + T_DEV], preferred_element_type=jnp.float32)
        weight_sum = weight_sum + rounded(partial_value)
    d_weight = weight_sum.astype(jnp.bfloat16)
    return (layer_out, d_query, d_key, d_value, d_weight)
```

```python
import functools
import math

import jax
import jax.numpy as jnp
from jax import lax
from jax.experimental import pallas as pl
from jax.experimental.pallas import tpu as pltpu
from jax.sharding import PartitionSpec as P

HD = 128
BLOCK = 128
FRAME_TOK = 384
PER_FRAME = FRAME_TOK // BLOCK
NZ = 4
NEG = -1e30
MESH = pl.DeviceIdType.MESH
VMEM = pl.BlockSpec(memory_space=pltpu.VMEM)
ANY = pl.BlockSpec(memory_space=pl.ANY)
f32 = jnp.float32
bf16 = jnp.bfloat16


def dot(a, b, ca, cb):
    return lax.dot_general(a, b, (((ca,), (cb,)), ((), ())), preferred_element_type=f32)


def line_barrier(nz, nx, z, x):
    barrier = pltpu.get_barrier_semaphore()
    for dz in range(1, nz):
        pl.semaphore_signal(
            barrier, inc=1, device_id={"seq": lax.rem(z + dz, nz) * nx + x}, device_id_type=MESH
        )
    for dx in range(1, nx):
        pl.semaphore_signal(
            barrier, inc=1, device_id={"seq": z * nx + lax.rem(x + dx, nx)}, device_id_type=MESH
        )
    pl.semaphore_wait(barrier, nz + nx - 2)


def gather_kernel(nz, nx, k_ref, v_ref, ko_ref, vo_ref, own_sem, zs, zr, xs, xr):
    me = lax.axis_index("seq")
    z, x = me // nx, lax.rem(me, nx)
    line_barrier(nz, nx, z, x)
    items = ((k_ref, ko_ref), (v_ref, vo_ref))
    started = []
    for i, (src, dst) in enumerate(items):
        for dx in range(1, nx):
            c = pltpu.make_async_remote_copy(
                src_ref=src, dst_ref=dst.at[me],
                send_sem=xs.at[i, 0, dx - 1], recv_sem=xr.at[i, 0, dx - 1],
                device_id={"seq": z * nx + lax.rem(x + dx, nx)}, device_id_type=MESH,
            )
            c.start()
            started.append(c)
        for dz in range(1, nz):
            c = pltpu.make_async_remote_copy(
                src_ref=src, dst_ref=dst.at[me],
                send_sem=zs.at[i, dz - 1], recv_sem=zr.at[i, dz - 1],
                device_id={"seq": lax.rem(z + dz, nz) * nx + x}, device_id_type=MESH,
            )
            c.start()
            started.append(c)
    own = []
    for i, (src, dst) in enumerate(items):
        c = pltpu.make_async_copy(src, dst.at[me], own_sem.at[i])
        c.start()
        own.append(c)
    for i, (src, dst) in enumerate(items):
        for dz in range(1, nz):
            s = lax.rem(z - dz + nz, nz) * nx + x
            pltpu.make_async_remote_copy(
                src_ref=src, dst_ref=dst.at[s],
                send_sem=zs.at[i, dz - 1], recv_sem=zr.at[i, dz - 1],
                device_id={"seq": s}, device_id_type=MESH,
            ).wait_recv()
            for dx in range(1, nx):
                c = pltpu.make_async_remote_copy(
                    src_ref=dst.at[s], dst_ref=dst.at[s],
                    send_sem=xs.at[i, dz, dx - 1], recv_sem=xr.at[i, dz, dx - 1],
                    device_id={"seq": z * nx + lax.rem(x + dx, nx)}, device_id_type=MESH,
                )
                c.start()
                started.append(c)
    for i, (src, dst) in enumerate(items):
        for dz in range(nz):
            for dx in range(1, nx):
                s = lax.rem(z - dz + nz, nz) * nx + lax.rem(x - dx + nx, nx)
                pltpu.make_async_remote_copy(
                    src_ref=src, dst_ref=dst.at[s],
                    send_sem=xs.at[i, dz, dx - 1], recv_sem=xr.at[i, dz, dx - 1],
                    device_id={"seq": z * nx + lax.rem(x + dx, nx)}, device_id_type=MESH,
                ).wait_recv()
    for c in started:
        c.wait_send()
    for c in own:
        c.wait()


def gather_rows(keys, values, n_seq):
    nz, nx = NZ, n_seq // NZ
    shape = jax.ShapeDtypeStruct((n_seq,) + keys.shape, keys.dtype)
    dma = pltpu.SemaphoreType.DMA
    return pl.pallas_call(
        functools.partial(gather_kernel, nz, nx),
        out_shape=(shape, shape),
        in_specs=[ANY, ANY],
        out_specs=(ANY, ANY),
        scratch_shapes=[
            dma((2,)), dma((2, nz - 1)), dma((2, nz - 1)), dma((2, nz, nx - 1)), dma((2, nz, nx - 1)),
        ],
        compiler_params=pltpu.CompilerParams(collective_id=0, has_side_effects=True),
    )(keys, values)


def scatter_kernel(nz, nx, scales, n, *refs):
    parts, outs = refs[:n], refs[n:2 * n]
    rx, sz, rz = refs[2 * n:3 * n], refs[3 * n:4 * n], refs[4 * n:5 * n]
    xs, xr, zs, zr = refs[5 * n:]
    me = lax.axis_index("seq")
    z, x = me // nx, lax.rem(me, nx)
    line_barrier(nz, nx, z, x)
    order = list(range(1, nz)) + [0]

    def piece(i, s):
        if len(parts[i].shape) == 3:
            return parts[i].at[s]
        width = outs[i].shape[1]
        return parts[i].at[:, pl.ds(pl.multiple_of(s * width, width), width)]

    def x_copy(i, dz, dx):
        px = lax.rem(x + dx, nx)
        return pltpu.make_async_remote_copy(
            src_ref=piece(i, lax.rem(z + dz, nz) * nx + px), dst_ref=rx[i].at[dz, dx - 1],
            send_sem=xs.at[i, dz, dx - 1], recv_sem=xr.at[i, dz, dx - 1],
            device_id={"seq": z * nx + px}, device_id_type=MESH,
        )

    def z_copy(i, dz):
        return pltpu.make_async_remote_copy(
            src_ref=sz[i].at[dz - 1], dst_ref=rz[i].at[dz - 1],
            send_sem=zs.at[i, dz - 1], recv_sem=zr.at[i, dz - 1],
            device_id={"seq": lax.rem(z + dz, nz) * nx + x}, device_id_type=MESH,
        )

    for i in range(n):
        for dz in order:
            for dx in range(1, nx):
                x_copy(i, dz, dx).start()
    for i in range(n):
        rows = outs[i].shape[0]
        for dz in order[:-1]:
            for dx in range(1, nx):
                x_copy(i, dz, dx).wait_recv()
            mine = piece(i, lax.rem(z + dz, nz) * nx + x)

            @pl.loop(0, rows // BLOCK)
            def _(r):
                at = pl.ds(pl.multiple_of(r * BLOCK, BLOCK), BLOCK)
                total = mine[at, :].astype(f32)
                for dx in range(1, nx):
                    total += rx[i][dz, dx - 1, at, :].astype(f32)
                sz[i][dz - 1, at, :] = total.astype(bf16)

            z_copy(i, dz).start()
    for i in range(n):
        rows = outs[i].shape[0]
        for dx in range(1, nx):
            x_copy(i, 0, dx).wait_recv()
        for dz in range(1, nz):
            z_copy(i, dz).wait_recv()
        mine = piece(i, me)

        @pl.loop(0, rows // BLOCK)
        def _(r):
            at = pl.ds(pl.multiple_of(r * BLOCK, BLOCK), BLOCK)
            total = mine[at, :].astype(f32)
            for dx in range(1, nx):
                total += rx[i][0, dx - 1, at, :].astype(f32)
            for dz in range(1, nz):
                total += rz[i][dz - 1, at, :].astype(f32)
            if scales[i] != 1.0:
                total = total * scales[i]
            outs[i][at, :] = total.astype(bf16)

    for i in range(n):
        for dz in range(nz):
            for dx in range(1, nx):
                x_copy(i, dz, dx).wait_send()
            if dz:
                z_copy(i, dz).wait_send()


def scatter_sum(parts, shapes, scales, n_seq, collective_id):
    nz, nx = NZ, n_seq // NZ
    n = len(parts)
    dma = pltpu.SemaphoreType.DMA
    return pl.pallas_call(
        functools.partial(scatter_kernel, nz, nx, scales, n),
        out_shape=tuple(jax.ShapeDtypeStruct(s, bf16) for s in shapes),
        in_specs=[VMEM] * n,
        out_specs=(VMEM,) * n,
        scratch_shapes=[pltpu.VMEM((nz, nx - 1) + s, bf16) for s in shapes]
        + [pltpu.VMEM((nz - 1,) + s, bf16) for s in shapes] * 2
        + [dma((n, nz, nx - 1)), dma((n, nz, nx - 1)), dma((n, nz - 1)), dma((n, nz - 1))],
        compiler_params=pltpu.CompilerParams(
            collective_id=collective_id, has_side_effects=True, vmem_limit_bytes=56 * 2**20
        ),
    )(*parts)


def attention_kernel(q_ref, k_ref, v_ref, g_ref, bias_ref, o_ref, dq_ref, dk_ref, dv_ref, e_ref):
    frames, rows, _ = k_ref.shape
    cols = q_ref.shape[0]
    scale = 1.0 / math.sqrt(HD)
    factor = scale * math.log2(math.e)
    q = q_ref[...]
    g = g_ref[...]

    def score_step(c, peak):
        s = dot(k_ref[c], q, 1, 1).reshape(PER_FRAME, BLOCK, cols) * factor
        s = (s + bias_ref[c][:, None, :]).reshape(rows, cols)
        e_ref[c] = s
        return jnp.maximum(peak, jnp.max(s.reshape(rows // 8, 8, cols), axis=0))

    peak = lax.fori_loop(0, frames, score_step, jnp.full((8, cols), NEG, f32))
    peak = jnp.max(peak, axis=0, keepdims=True)

    def sum_step(c, carry):
        total, out = carry
        e = jnp.exp2(e_ref[c] - peak)
        e_ref[c] = e
        total = total + jnp.sum(e.reshape(rows // 8, 8, cols), axis=0)
        out = out + dot(v_ref[c], e.astype(bf16), 0, 0)
        return total, out

    total, out = lax.fori_loop(
        0, frames, sum_step, (jnp.zeros((8, cols), f32), jnp.zeros((HD, cols), f32))
    )
    inverse = 1.0 / jnp.sum(total, axis=0, keepdims=True)
    out = (out * inverse).astype(bf16).astype(f32)
    o_ref[...] = out.T.astype(bf16)
    delta = jnp.sum(g.astype(f32).T * out, axis=0, keepdims=True)

    def grad_step(c, dq):
        w = e_ref[c] * inverse
        dv_ref[c] = dot(w.astype(bf16), g, 1, 0).astype(bf16)
        gw = dot(v_ref[c], g, 1, 1)
        ds = (w * (gw - delta)).astype(bf16)
        dk_ref[c] = dot(ds, q, 1, 0).astype(bf16)
        return dq + dot(k_ref[c], ds, 0, 0)

    dq = lax.fori_loop(0, frames, grad_step, jnp.zeros((HD, cols), f32))
    dq_ref[...] = (dq * scale).T.astype(bf16)


def attention(queries, keys, values, grads, bias):
    rows, width = queries.shape
    heads = width // HD
    by_head = pl.BlockSpec((rows, HD), lambda h: (0, h))
    whole = pl.BlockSpec((keys.shape[0], keys.shape[1], HD), lambda h: (0, 0, h))
    flops = 12 * rows * keys.shape[0] * keys.shape[1] * width
    return pl.pallas_call(
        attention_kernel,
        grid=(heads,),
        out_shape=(
            jax.ShapeDtypeStruct(queries.shape, bf16),
            jax.ShapeDtypeStruct(queries.shape, bf16),
            jax.ShapeDtypeStruct(keys.shape, bf16),
            jax.ShapeDtypeStruct(keys.shape, bf16),
        ),
        in_specs=[by_head, whole, whole, by_head, pl.BlockSpec(bias.shape, lambda h: (0, 0, 0))],
        out_specs=(by_head, by_head, whole, whole),
        scratch_shapes=[pltpu.VMEM((keys.shape[0], keys.shape[1], rows), f32)],
        compiler_params=pltpu.CompilerParams(vmem_limit_bytes=56 * 2**20),
        cost_estimate=pl.CostEstimate(
            flops=flops, bytes_accessed=4 * 2 * keys.size, transcendentals=flops // (12 * HD)
        ),
    )(queries, keys, values, grads, bias)


def mask_bias(block_keys, key_count, frame_slot, seq_index, local_blocks):
    frames = frame_slot.shape[0]
    block_count, entries_count = block_keys.shape
    ids = jnp.arange(frames, dtype=jnp.int32)
    local_frames = local_blocks // PER_FRAME
    slots = seq_index * local_frames + jnp.arange(local_frames, dtype=jnp.int32)
    frame_at = jnp.sum(jnp.where(frame_slot[None, :] == slots[:, None], ids[None, :], 0), axis=1)
    logical = (frame_at[:, None] * PER_FRAME + jnp.arange(PER_FRAME)[None, :]).reshape(-1)
    all_blocks = jnp.arange(block_count, dtype=jnp.int32)
    pick = logical[:, None] == all_blocks[None, :]
    entries = jnp.sum(jnp.where(pick[:, :, None], block_keys[None], 0), axis=1)
    counts = jnp.sum(jnp.where(pick, key_count[None, :], 0), axis=1)
    slot_of = jnp.sum(
        jnp.where((entries // PER_FRAME)[..., None] == ids, frame_slot, 0), axis=-1
    )
    stored = slot_of * PER_FRAME + entries % PER_FRAME
    attended = jnp.arange(entries_count)[None, :] < counts[:, None]
    hit = jnp.any((stored[..., None] == all_blocks) & attended[..., None], axis=1)
    bias = jnp.where(hit, 0.0, NEG).astype(f32).T
    return jnp.repeat(bias, BLOCK, axis=1).reshape(frames, PER_FRAME, local_blocks * BLOCK)


def on_device(n_seq, queries, keys, values, out_weight, d_output, block_keys, key_count, frame_slot):
    rows, width = queries.shape
    seq_index = lax.axis_index("seq")
    bias = mask_bias(block_keys, key_count, frame_slot, seq_index, rows // BLOCK)
    full_grad = lax.all_gather(d_output, "head", axis=1, tiled=True)
    all_keys, all_values = gather_rows(keys, values, n_seq)
    d_attn = dot(full_grad, out_weight, 1, 1).astype(bf16)
    attn, d_query, key_parts, value_parts = attention(queries, all_keys, all_values, d_attn, bias)
    layer_out = lax.psum_scatter(
        dot(attn, out_weight, 1, 0).astype(bf16), "head", scatter_dimension=1, tiled=True
    )
    weight_part = dot(attn, full_grad, 0, 0).astype(bf16)
    share = out_weight.shape[1] // n_seq
    if share % 128:
        weight_part = weight_part.reshape(width, n_seq, share).transpose(1, 0, 2)
    d_key, d_value, d_weight = scatter_sum(
        (key_parts, value_parts, weight_part),
        ((rows, width), (rows, width), (width, share)),
        (1.0 / math.sqrt(HD), 1.0, 1.0),
        n_seq,
        1,
    )
    return (layer_out, d_query, d_key, d_value, d_weight)


def solution(mesh):
    return jax.shard_map(
        functools.partial(on_device, mesh.shape["seq"]),
        mesh=mesh,
        in_specs=(
            P("seq", "head"),
            P("seq", "head"),
            P("seq", "head"),
            P("head", None),
            P("seq", "head"),
            P(),
            P(),
            P(),
        ),
        out_specs=(
            P("seq", "head"),
            P("seq", "head"),
            P("seq", "head"),
            P("seq", "head"),
            P("head", "seq"),
        ),
        check_vma=False,
    )
```

```python
import functools
import math

import jax
import jax.numpy as jnp
from jax import lax
from jax.experimental import pallas as pl
from jax.experimental.pallas import tpu as pltpu
from jax.sharding import PartitionSpec as P

HD = 128
BLOCK = 128
FRAME_TOK = 384
PER_FRAME = FRAME_TOK // BLOCK
NZ = 4
NEG = -1e30
MESH = pl.DeviceIdType.MESH
VMEM = pl.BlockSpec(memory_space=pltpu.VMEM)
ANY = pl.BlockSpec(memory_space=pl.ANY)
f32 = jnp.float32
bf16 = jnp.bfloat16


def dot(a, b, ca, cb):
    return lax.dot_general(a, b, (((ca,), (cb,)), ((), ())), preferred_element_type=f32)


def line_barrier(nz, nx, z, x):
    barrier = pltpu.get_barrier_semaphore()
    for dz in range(1, nz):
        pl.semaphore_signal(
            barrier, inc=1, device_id={"seq": lax.rem(z + dz, nz) * nx + x}, device_id_type=MESH
        )
    for dx in range(1, nx):
        pl.semaphore_signal(
            barrier, inc=1, device_id={"seq": z * nx + lax.rem(x + dx, nx)}, device_id_type=MESH
        )
    pl.semaphore_wait(barrier, nz + nx - 2)


def gather_kernel(nz, nx, k_ref, v_ref, ko_ref, vo_ref, own_sem, zs, zr, xs, xr):
    me = lax.axis_index("seq")
    z, x = me // nx, lax.rem(me, nx)
    line_barrier(nz, nx, z, x)
    items = ((k_ref, ko_ref), (v_ref, vo_ref))
    started = []
    for i, (src, dst) in enumerate(items):
        for dx in range(1, nx):
            c = pltpu.make_async_remote_copy(
                src_ref=src, dst_ref=dst.at[me],
                send_sem=xs.at[i, 0, dx - 1], recv_sem=xr.at[i, 0, dx - 1],
                device_id={"seq": z * nx + lax.rem(x + dx, nx)}, device_id_type=MESH,
            )
            c.start()
            started.append(c)
        for dz in range(1, nz):
            c = pltpu.make_async_remote_copy(
                src_ref=src, dst_ref=dst.at[me],
                send_sem=zs.at[i, dz - 1], recv_sem=zr.at[i, dz - 1],
                device_id={"seq": lax.rem(z + dz, nz) * nx + x}, device_id_type=MESH,
            )
            c.start()
            started.append(c)
    own = []
    for i, (src, dst) in enumerate(items):
        c = pltpu.make_async_copy(src, dst.at[me], own_sem.at[i])
        c.start()
        own.append(c)
    for i, (src, dst) in enumerate(items):
        for dz in range(1, nz):
            s = lax.rem(z - dz + nz, nz) * nx + x
            pltpu.make_async_remote_copy(
                src_ref=src, dst_ref=dst.at[s],
                send_sem=zs.at[i, dz - 1], recv_sem=zr.at[i, dz - 1],
                device_id={"seq": s}, device_id_type=MESH,
            ).wait_recv()
            for dx in range(1, nx):
                c = pltpu.make_async_remote_copy(
                    src_ref=dst.at[s], dst_ref=dst.at[s],
                    send_sem=xs.at[i, dz, dx - 1], recv_sem=xr.at[i, dz, dx - 1],
                    device_id={"seq": z * nx + lax.rem(x + dx, nx)}, device_id_type=MESH,
                )
                c.start()
                started.append(c)
    for i, (src, dst) in enumerate(items):
        for dz in range(nz):
            for dx in range(1, nx):
                s = lax.rem(z - dz + nz, nz) * nx + lax.rem(x - dx + nx, nx)
                pltpu.make_async_remote_copy(
                    src_ref=src, dst_ref=dst.at[s],
                    send_sem=xs.at[i, dz, dx - 1], recv_sem=xr.at[i, dz, dx - 1],
                    device_id={"seq": z * nx + lax.rem(x + dx, nx)}, device_id_type=MESH,
                ).wait_recv()
    for c in started:
        c.wait_send()
    for c in own:
        c.wait()


def gather_rows(keys, values, n_seq):
    nz, nx = NZ, n_seq // NZ
    shape = jax.ShapeDtypeStruct((n_seq,) + keys.shape, keys.dtype)
    dma = pltpu.SemaphoreType.DMA
    return pl.pallas_call(
        functools.partial(gather_kernel, nz, nx),
        out_shape=(shape, shape),
        in_specs=[ANY, ANY],
        out_specs=(ANY, ANY),
        scratch_shapes=[
            dma((2,)), dma((2, nz - 1)), dma((2, nz - 1)), dma((2, nz, nx - 1)), dma((2, nz, nx - 1)),
        ],
        compiler_params=pltpu.CompilerParams(collective_id=0, has_side_effects=True),
    )(keys, values)


def head(h):
    return slice(h * HD, (h + 1) * HD)


def forward_kernel(q_ref, k_ref, v_ref, bias_ref, o_ref, ot_ref, lse_ref, e_ref):
    frames, rows, _ = k_ref.shape
    cols = q_ref.shape[0]
    q = q_ref[...]

    def score_step(c, peak):
        s = scores(k_ref[c], q, bias_ref[c])
        e_ref[c] = s
        return jnp.maximum(peak, jnp.max(s.reshape(rows // 8, 8, cols), axis=0))

    peak = lax.fori_loop(0, frames, score_step, jnp.full((8, cols), NEG, f32))
    peak = jnp.max(peak, axis=0, keepdims=True)

    def sum_step(c, carry):
        total, out = carry
        e = jnp.exp2(e_ref[c] - peak)
        total = total + jnp.sum(e.reshape(rows // 8, 8, cols), axis=0)
        out = out + dot(v_ref[c], e.astype(bf16), 0, 0)
        return total, out

    total, out = lax.fori_loop(
        0, frames, sum_step, (jnp.zeros((8, cols), f32), jnp.zeros((HD, cols), f32))
    )
    total = jnp.sum(total, axis=0, keepdims=True)
    out = out / total
    ot_ref[...] = out.astype(bf16)
    o_ref[...] = out.T.astype(bf16)
    lse_ref[0] = jnp.broadcast_to(peak + jnp.log2(total), (8, cols))


def scores(k, q, bias):
    rows, cols = k.shape[0], q.shape[0]
    factor = math.log2(math.e) / math.sqrt(HD)
    s = dot(k, q, 1, 1).reshape(PER_FRAME, BLOCK, cols) * factor
    return (s + bias[:, None, :]).reshape(rows, cols)


def forward(queries, keys, values, bias):
    rows, width = queries.shape
    heads = width // HD
    by_head = pl.BlockSpec((rows, HD), lambda h: (0, h))
    whole = pl.BlockSpec((keys.shape[0], keys.shape[1], HD), lambda h: (0, 0, h))
    flops = 4 * rows * keys.size
    return pl.pallas_call(
        forward_kernel,
        grid=(heads,),
        out_shape=(
            jax.ShapeDtypeStruct(queries.shape, bf16),
            jax.ShapeDtypeStruct((width, rows), bf16),
            jax.ShapeDtypeStruct((heads, 8, rows), f32),
        ),
        in_specs=[by_head, whole, whole, pl.BlockSpec(bias.shape, lambda h: (0, 0, 0))],
        out_specs=(
            by_head,
            pl.BlockSpec((HD, rows), lambda h: (h, 0)),
            pl.BlockSpec((1, 8, rows), lambda h: (h, 0, 0)),
        ),
        scratch_shapes=[pltpu.VMEM((keys.shape[0], keys.shape[1], rows), f32)],
        compiler_params=pltpu.CompilerParams(vmem_limit_bytes=48 * 2**20),
        cost_estimate=pl.CostEstimate(
            flops=flops, bytes_accessed=4 * keys.size, transcendentals=flops // (4 * HD)
        ),
    )(queries, keys, values, bias)


def backward_kernel(
    nz, nx, nh,
    q_ref, k_ref, v_ref, o_ref, ot_ref, lse_ref, bias_ref, grad_ref, ow_ref,
    layer_ref, dq_ref, dk_ref, dv_ref, dw_ref,
    wp, kp, vp, wx, kx, vx, wz, kz, vz, lp, lr, g_ref, acc, stat,
    xs, xr, zs, zr, ls, lrs,
):
    me = lax.axis_index("seq")
    hd = lax.axis_index("head")
    z, x = me // nx, lax.rem(me, nx)
    n_seq = nz * nx
    rows, width = q_ref.shape
    heads = width // HD
    scale = 1.0 / math.sqrt(HD)
    parts, rx, rz, outs = (wp, kp, vp), (wx, kx, vx), (wz, kz, vz), (dw_ref, dk_ref, dv_ref)

    barrier = pltpu.get_barrier_semaphore()
    for dz in range(1, nz):
        pl.semaphore_signal(
            barrier, inc=1, device_id={"seq": lax.rem(z + dz, nz) * nx + x}, device_id_type=MESH
        )
    for dx in range(1, nx):
        pl.semaphore_signal(
            barrier, inc=1, device_id={"seq": z * nx + lax.rem(x + dx, nx)}, device_id_type=MESH
        )
    for dh in range(1, nh):
        pl.semaphore_signal(
            barrier, inc=1, device_id={"head": lax.rem(hd + dh, nh)}, device_id_type=MESH
        )
    pl.semaphore_wait(barrier, nz + nx + nh - 3)

    def x_copy(i, dz, dx):
        px = lax.rem(x + dx, nx)
        return pltpu.make_async_remote_copy(
            src_ref=parts[i].at[lax.rem(z + dz, nz) * nx + px], dst_ref=rx[i].at[dz, dx - 1],
            send_sem=xs.at[i, dz, dx - 1], recv_sem=xr.at[i, dz, dx - 1],
            device_id={"seq": z * nx + px}, device_id_type=MESH,
        )

    def z_copy(i, dz):
        to = lax.rem(z + dz, nz) * nx + x
        return pltpu.make_async_remote_copy(
            src_ref=parts[i].at[to], dst_ref=rz[i].at[dz - 1],
            send_sem=zs.at[i, dz - 1], recv_sem=zr.at[i, dz - 1],
            device_id={"seq": to}, device_id_type=MESH,
        )

    def l_copy(dh):
        return pltpu.make_async_remote_copy(
            src_ref=lp.at[dh], dst_ref=lr.at[dh - 1],
            send_sem=ls.at[dh - 1], recv_sem=lrs.at[dh - 1],
            device_id={"head": lax.rem(hd + dh, nh)}, device_id_type=MESH,
        )

    def step(u):
        dz = lax.rem(u // nx + 1, nz)
        dx = lax.rem(lax.rem(u, nx) + 1, nx)
        return dz, dx, lax.rem(z + dz, nz) * nx + lax.rem(x + dx, nx)

    def forward_sum(i, dz):
        for dx in range(1, nx):
            x_copy(i, dz, dx).wait_recv()
        s = lax.rem(z + dz, nz) * nx + x

        @pl.loop(0, outs[i].shape[0] // BLOCK)
        def _(r):
            at = pl.ds(pl.multiple_of(r * BLOCK, BLOCK), BLOCK)
            total = parts[i][s, at, :].astype(f32)
            for dx in range(1, nx):
                total += rx[i][dz, dx - 1, at, :].astype(f32)
            parts[i][s, at, :] = total.astype(bf16)

        z_copy(i, dz).start()

    def last_sum(i, factor):
        for dx in range(1, nx):
            x_copy(i, 0, dx).wait_recv()
        for dz in range(1, nz):
            z_copy(i, dz).wait_recv()

        @pl.loop(0, outs[i].shape[0] // BLOCK)
        def _(r):
            at = pl.ds(pl.multiple_of(r * BLOCK, BLOCK), BLOCK)
            total = parts[i][me, at, :].astype(f32)
            for dx in range(1, nx):
                total += rx[i][0, dx - 1, at, :].astype(f32)
            for dz in range(1, nz):
                total += rz[i][dz - 1, at, :].astype(f32)
            outs[i][at, :] = (total * factor).astype(bf16)

    share = dw_ref.shape[1]
    group = math.lcm(share, 128) // share

    def weight_part(p):
        span = group * share
        r = jnp.dot(
            ot_ref[...],
            grad_ref[:, pl.ds(pl.multiple_of(p * span, 128), span)],
            preferred_element_type=f32,
        ).astype(bf16)
        for t in range(group):
            wp[p * group + t] = r[:, t * share:(t + 1) * share]

    if group > 1:
        pl.loop(0, n_seq // group)(weight_part)

    @pl.loop(0, n_seq)
    def _(u):
        dz, dx, s = step(u)
        if group == 1:
            weight_part(s)

        @pl.when(dx > 0)
        def _():
            x_copy(0, dz, dx).start()

    lw = layer_ref.shape[1]

    @pl.loop(0, nh)
    def _(j):
        dh = lax.rem(j + 1, nh)
        at = pl.ds(pl.multiple_of(lax.rem(hd + dh, nh) * lw, 128), lw)
        lp[dh] = jnp.dot(o_ref[...], ow_ref[:, at], preferred_element_type=f32).astype(bf16)

        @pl.when(dh > 0)
        def _():
            l_copy(dh).start()

    acc[...] = jnp.zeros_like(acc)
    chunk = 640

    @pl.loop(0, grad_ref.shape[1] // chunk)
    def _(c):
        at = pl.ds(pl.multiple_of(c * chunk, 128), chunk)
        acc[...] += dot(grad_ref[:, at], ow_ref[:, at], 1, 1)

    g_ref[...] = acc[...].astype(bf16)
    acc[...] = jnp.zeros_like(acc)
    for h in range(heads):
        gt = g_ref[:, head(h)].astype(f32).T
        stat[h] = jnp.broadcast_to(
            jnp.sum(gt * ot_ref[head(h), :].astype(f32), axis=0, keepdims=True), (8, rows)
        )

    @pl.loop(0, n_seq)
    def _(u):
        dz, dx, s = step(u)
        for h in range(heads):
            q, g = q_ref[:, head(h)], g_ref[:, head(h)]
            k, v = k_ref[s, :, head(h)], v_ref[s, :, head(h)]
            w = jnp.exp2(scores(k, q, bias_ref[s]) - lse_ref[h, 0:1, :])
            vp[s, :, head(h)] = dot(w.astype(bf16), g, 1, 0).astype(bf16)
            ds = (w * (dot(v, g, 1, 1) - stat[h, 0:1, :])).astype(bf16)
            kp[s, :, head(h)] = dot(ds, q, 1, 0).astype(bf16)
            acc[head(h), :] += dot(k, ds, 0, 0)

        @pl.when(dx > 0)
        def _():
            x_copy(1, dz, dx).start()
            x_copy(2, dz, dx).start()

        @pl.when((dx == 0) & (dz > 0))
        def _():
            forward_sum(0, dz)

    dq_ref[...] = (acc[...] * scale).T.astype(bf16)

    @pl.loop(1, nz)
    def _(dz):
        forward_sum(1, dz)
        forward_sum(2, dz)

    @pl.loop(1, nh)
    def _(dh):
        l_copy(dh).wait_recv()

    @pl.loop(0, rows // BLOCK)
    def _(r):
        at = pl.ds(pl.multiple_of(r * BLOCK, BLOCK), BLOCK)
        total = lp[0, at, :].astype(f32)
        for dh in range(1, nh):
            total += lr[dh - 1, at, :].astype(f32)
        layer_ref[at, :] = total.astype(bf16)

    last_sum(0, 1.0)
    last_sum(1, scale)
    last_sum(2, 1.0)
    for i in range(3):
        for dz in range(nz):
            for dx in range(1, nx):
                x_copy(i, dz, dx).wait_send()
            if dz:
                z_copy(i, dz).wait_send()
    for dh in range(1, nh):
        l_copy(dh).wait_send()


def backward(n_seq, nh, queries, keys, values, attn, attn_t, lse, bias, full_grad, out_weight):
    nz, nx = NZ, n_seq // NZ
    rows, width = queries.shape
    columns = out_weight.shape[1]
    shapes = ((width, columns // n_seq), (rows, width), (rows, width))
    dma = pltpu.SemaphoreType.DMA
    x_sem, z_sem, l_sem = dma((3, nz, nx - 1)), dma((3, nz - 1)), dma((nh - 1,))
    one = jax.ShapeDtypeStruct((rows, width), bf16)
    return pl.pallas_call(
        functools.partial(backward_kernel, nz, nx, nh),
        out_shape=(
            jax.ShapeDtypeStruct((rows, columns // nh), bf16),
            one,
            one,
            one,
            jax.ShapeDtypeStruct(shapes[0], bf16),
        ),
        in_specs=[VMEM] * 9,
        out_specs=(VMEM,) * 5,
        scratch_shapes=[pltpu.VMEM((n_seq,) + s, bf16) for s in shapes]
        + [pltpu.VMEM((nz, nx - 1) + s, bf16) for s in shapes]
        + [pltpu.VMEM((nz - 1,) + s, bf16) for s in shapes]
        + [
            pltpu.VMEM((nh, rows, columns // nh), bf16),
            pltpu.VMEM((nh - 1, rows, columns // nh), bf16),
            pltpu.VMEM((rows, width), bf16),
            pltpu.VMEM((width, rows), f32),
            pltpu.VMEM((width // HD, 8, rows), f32),
        ]
        + [x_sem, x_sem, z_sem, z_sem, l_sem, l_sem],
        compiler_params=pltpu.CompilerParams(
            collective_id=1, has_side_effects=True, vmem_limit_bytes=60 * 2**20
        ),
    )(queries, keys, values, attn, attn_t, lse, bias, full_grad, out_weight)


def mask_bias(block_keys, key_count, frame_slot, seq_index, local_blocks):
    frames = frame_slot.shape[0]
    block_count, entries_count = block_keys.shape
    ids = jnp.arange(frames, dtype=jnp.int32)
    local_frames = local_blocks // PER_FRAME
    slots = seq_index * local_frames + jnp.arange(local_frames, dtype=jnp.int32)
    frame_at = jnp.sum(jnp.where(frame_slot[None, :] == slots[:, None], ids[None, :], 0), axis=1)
    logical = (frame_at[:, None] * PER_FRAME + jnp.arange(PER_FRAME)[None, :]).reshape(-1)
    all_blocks = jnp.arange(block_count, dtype=jnp.int32)
    pick = logical[:, None] == all_blocks[None, :]
    entries = jnp.sum(jnp.where(pick[:, :, None], block_keys[None], 0), axis=1)
    counts = jnp.sum(jnp.where(pick, key_count[None, :], 0), axis=1)
    slot_of = jnp.sum(
        jnp.where((entries // PER_FRAME)[..., None] == ids, frame_slot, 0), axis=-1
    )
    stored = slot_of * PER_FRAME + entries % PER_FRAME
    attended = jnp.arange(entries_count)[None, :] < counts[:, None]
    hit = jnp.any((stored[..., None] == all_blocks) & attended[..., None], axis=1)
    bias = jnp.where(hit, 0.0, NEG).astype(f32).T
    return jnp.repeat(bias, BLOCK, axis=1).reshape(frames, PER_FRAME, local_blocks * BLOCK)


def on_device(
    n_seq, n_head,
    queries, keys, values, out_weight, d_output, block_keys, key_count, frame_slot,
):
    rows, width = queries.shape
    seq_index = lax.axis_index("seq")
    bias = mask_bias(block_keys, key_count, frame_slot, seq_index, rows // BLOCK)
    full_grad = lax.all_gather(d_output, "head", axis=1, tiled=True)
    all_keys, all_values = gather_rows(keys, values, n_seq)
    attn, attn_t, lse = forward(queries, all_keys, all_values, bias)
    return backward(
        n_seq, n_head, queries, all_keys, all_values, attn, attn_t, lse, bias, full_grad, out_weight
    )


def solution(mesh):
    return jax.shard_map(
        functools.partial(on_device, mesh.shape["seq"], mesh.shape["head"]),
        mesh=mesh,
        in_specs=(
            P("seq", "head"),
            P("seq", "head"),
            P("seq", "head"),
            P("head", None),
            P("seq", "head"),
            P(),
            P(),
            P(),
        ),
        out_specs=(
            P("seq", "head"),
            P("seq", "head"),
            P("seq", "head"),
            P("seq", "head"),
            P("head", "seq"),
        ),
        check_vma=False,
    )
```

```python
import functools
import math

import jax
import jax.numpy as jnp
from jax import lax
from jax.experimental import pallas as pl
from jax.experimental.pallas import tpu as pltpu
from jax.sharding import PartitionSpec as P

HD = 128
BLOCK = 128
FRAME_TOK = 384
PER_FRAME = FRAME_TOK // BLOCK
NZ = 4
NEG = -1e30
MESH = pl.DeviceIdType.MESH
VMEM = pl.BlockSpec(memory_space=pltpu.VMEM)
ANY = pl.BlockSpec(memory_space=pl.ANY)
f32 = jnp.float32
bf16 = jnp.bfloat16


def dot(a, b, ca, cb):
    return lax.dot_general(a, b, (((ca,), (cb,)), ((), ())), preferred_element_type=f32)


def line_barrier(nz, nx, z, x):
    barrier = pltpu.get_barrier_semaphore()
    for dz in range(1, nz):
        pl.semaphore_signal(
            barrier, inc=1, device_id={"seq": lax.rem(z + dz, nz) * nx + x}, device_id_type=MESH
        )
    for dx in range(1, nx):
        pl.semaphore_signal(
            barrier, inc=1, device_id={"seq": z * nx + lax.rem(x + dx, nx)}, device_id_type=MESH
        )
    pl.semaphore_wait(barrier, nz + nx - 2)


def gather_kernel(nz, nx, k_ref, v_ref, ko_ref, vo_ref, own_sem, zs, zr, xs, xr):
    me = lax.axis_index("seq")
    z, x = me // nx, lax.rem(me, nx)
    line_barrier(nz, nx, z, x)
    items = ((k_ref, ko_ref), (v_ref, vo_ref))
    sides = ((0, 1), (1, -1))

    def x_copy(i, zz, px, dx, source):
        shard = items[i][1].at[zz * nx + px]
        return pltpu.make_async_remote_copy(
            src_ref=shard if source is None else source, dst_ref=shard,
            send_sem=xs.at[i, zz, dx - 1], recv_sem=xr.at[i, zz, dx - 1],
            device_id={"seq": z * nx + lax.rem(x + dx, nx)}, device_id_type=MESH,
        )

    def z_copy(i, side, way, d, origin, source):
        shard = items[i][1].at[origin * nx + x]
        return pltpu.make_async_remote_copy(
            src_ref=shard if source is None else source, dst_ref=shard,
            send_sem=zs.at[i, side, d - 1], recv_sem=zr.at[i, side, d - 1],
            device_id={"seq": lax.rem(z + way + nz, nz) * nx + x}, device_id_type=MESH,
        )

    def inside(p):
        return (p >= 0) & (p < nz)

    for i in range(2):
        for side, way in sides:
            @pl.when(inside(z + way))
            def _():
                z_copy(i, side, way, 1, z, items[i][0]).start()
        for dx in range(1, nx):
            x_copy(i, z, x, dx, items[i][0]).start()
        pltpu.make_async_copy(items[i][0], items[i][1].at[me], own_sem.at[i]).start()
    for d in range(1, nz):
        for i in range(2):
            for side, way in sides:
                origin = z - way * d

                @pl.when(inside(origin))
                def _():
                    z_copy(i, side, way, d, origin, None).wait_recv()
                    if d + 1 < nz:
                        @pl.when(inside(z + way))
                        def _():
                            z_copy(i, side, way, d + 1, origin, None).start()
                    for dx in range(1, nx):
                        x_copy(i, origin, x, dx, None).start()
    for i in range(2):
        for zz in range(nz):
            for dx in range(1, nx):
                x_copy(i, zz, lax.rem(x - dx + nx, nx), dx, None).wait_recv()
    for i in range(2):
        for zz in range(nz):
            for dx in range(1, nx):
                x_copy(i, zz, x, dx, None).wait_send()
        for d in range(1, nz):
            for side, way in sides:
                origin = z - way * (d - 1)

                @pl.when(inside(origin) & inside(z + way))
                def _():
                    z_copy(i, side, way, d, origin, None).wait_send()
        pltpu.make_async_copy(items[i][0], items[i][1].at[me], own_sem.at[i]).wait()


def gather_rows(keys, values, n_seq):
    nz, nx = NZ, n_seq // NZ
    shape = jax.ShapeDtypeStruct((n_seq,) + keys.shape, keys.dtype)
    dma = pltpu.SemaphoreType.DMA
    z_sem, x_sem = dma((2, 2, nz - 1)), dma((2, nz, nx - 1))
    return pl.pallas_call(
        functools.partial(gather_kernel, nz, nx),
        out_shape=(shape, shape),
        in_specs=[VMEM, VMEM],
        out_specs=(VMEM, VMEM),
        scratch_shapes=[dma((2,)), z_sem, z_sem, x_sem, x_sem],
        compiler_params=pltpu.CompilerParams(
            collective_id=0, has_side_effects=True, vmem_limit_bytes=24 * 2**20
        ),
    )(keys, values)


def store_kernel(n, *refs):
    sems = refs[2 * n]
    copies = [pltpu.make_async_copy(refs[i], refs[n + i], sems.at[i]) for i in range(n)]
    for c in copies:
        c.start()
    for c in copies:
        c.wait()


def store(arrays):
    n = len(arrays)
    return pl.pallas_call(
        functools.partial(store_kernel, n),
        out_shape=tuple(jax.ShapeDtypeStruct(a.shape, a.dtype) for a in arrays),
        in_specs=[VMEM] * n,
        out_specs=(ANY,) * n,
        scratch_shapes=[pltpu.SemaphoreType.DMA((n,))],
    )(*arrays)


def head(h):
    return slice(h * HD, (h + 1) * HD)


def forward_kernel(q_ref, k_ref, v_ref, bias_ref, o_ref, ot_ref, lse_ref, e_ref):
    frames, rows, _ = k_ref.shape
    cols = q_ref.shape[0]
    q = q_ref[...]

    def score_step(c, peak):
        s = scores(k_ref[c], q, bias_ref[c])
        e_ref[c] = s
        return jnp.maximum(peak, jnp.max(s.reshape(rows // 8, 8, cols), axis=0))

    peak = lax.fori_loop(0, frames, score_step, jnp.full((8, cols), NEG, f32))
    peak = jnp.max(peak, axis=0, keepdims=True)

    def sum_step(c, carry):
        total, out = carry
        e = jnp.exp2(e_ref[c] - peak)
        total = total + jnp.sum(e.reshape(rows // 8, 8, cols), axis=0)
        out = out + dot(v_ref[c], e.astype(bf16), 0, 0)
        return total, out

    total, out = lax.fori_loop(
        0, frames, sum_step, (jnp.zeros((8, cols), f32), jnp.zeros((HD, cols), f32))
    )
    total = jnp.sum(total, axis=0, keepdims=True)
    out = out / total
    ot_ref[...] = out.astype(bf16)
    o_ref[...] = out.T.astype(bf16)
    lse_ref[0] = jnp.broadcast_to(peak + jnp.log2(total), (8, cols))


def scores(k, q, bias):
    rows, cols = k.shape[0], q.shape[0]
    factor = math.log2(math.e) / math.sqrt(HD)
    s = dot(k, q, 1, 1).reshape(PER_FRAME, BLOCK, cols) * factor
    return (s + bias[:, None, :]).reshape(rows, cols)


def forward(queries, keys, values, bias):
    rows, width = queries.shape
    heads = width // HD
    by_head = pl.BlockSpec((rows, HD), lambda h: (0, h))
    whole = pl.BlockSpec((keys.shape[0], keys.shape[1], HD), lambda h: (0, 0, h))
    flops = 4 * rows * keys.size
    return pl.pallas_call(
        forward_kernel,
        grid=(heads,),
        out_shape=(
            jax.ShapeDtypeStruct(queries.shape, bf16),
            jax.ShapeDtypeStruct((width, rows), bf16),
            jax.ShapeDtypeStruct((heads, 8, rows), f32),
        ),
        in_specs=[by_head, whole, whole, pl.BlockSpec(bias.shape, lambda h: (0, 0, 0))],
        out_specs=(
            by_head,
            pl.BlockSpec((HD, rows), lambda h: (h, 0)),
            pl.BlockSpec((1, 8, rows), lambda h: (h, 0, 0)),
        ),
        scratch_shapes=[pltpu.VMEM((keys.shape[0], keys.shape[1], rows), f32)],
        compiler_params=pltpu.CompilerParams(vmem_limit_bytes=24 * 2**20),
        cost_estimate=pl.CostEstimate(
            flops=flops, bytes_accessed=4 * keys.size, transcendentals=flops // (4 * HD)
        ),
    )(queries, keys, values, bias)


def backward_kernel(
    nz, nx, nh,
    q_ref, k_ref, v_ref, o_ref, ot_ref, lse_ref, bias_ref, grad_ref, ow_ref,
    layer_ref, dq_ref, dk_ref, dv_ref, dw_ref,
    wp, kp, vp, wx, kx, vx, wz, kz, vz, lp, lr, g_ref, acc, stat,
    xs, xr, zs, zr, ls, lrs,
):
    me = lax.axis_index("seq")
    hd = lax.axis_index("head")
    z, x = me // nx, lax.rem(me, nx)
    n_seq = nz * nx
    rows, width = q_ref.shape
    heads = width // HD
    scale = 1.0 / math.sqrt(HD)
    parts, rx, rz, outs = (wp, kp, vp), (wx, kx, vx), (wz, kz, vz), (dw_ref, dk_ref, dv_ref)

    barrier = pltpu.get_barrier_semaphore()
    for dz in range(1, nz):
        pl.semaphore_signal(
            barrier, inc=1, device_id={"seq": lax.rem(z + dz, nz) * nx + x}, device_id_type=MESH
        )
    for dx in range(1, nx):
        pl.semaphore_signal(
            barrier, inc=1, device_id={"seq": z * nx + lax.rem(x + dx, nx)}, device_id_type=MESH
        )
    for dh in range(1, nh):
        pl.semaphore_signal(
            barrier, inc=1, device_id={"head": lax.rem(hd + dh, nh)}, device_id_type=MESH
        )
    pl.semaphore_wait(barrier, nz + nx + nh - 3)

    def x_copy(i, dz, dx):
        px = lax.rem(x + dx, nx)
        return pltpu.make_async_remote_copy(
            src_ref=parts[i].at[lax.rem(z + dz, nz) * nx + px], dst_ref=rx[i].at[dz, dx - 1],
            send_sem=xs.at[i, dz, dx - 1], recv_sem=xr.at[i, dz, dx - 1],
            device_id={"seq": z * nx + px}, device_id_type=MESH,
        )

    def z_copy(i, dz):
        to = lax.rem(z + dz, nz) * nx + x
        return pltpu.make_async_remote_copy(
            src_ref=parts[i].at[to], dst_ref=rz[i].at[dz - 1],
            send_sem=zs.at[i, dz - 1], recv_sem=zr.at[i, dz - 1],
            device_id={"seq": to}, device_id_type=MESH,
        )

    def l_copy(dh):
        return pltpu.make_async_remote_copy(
            src_ref=lp.at[dh], dst_ref=lr.at[dh - 1],
            send_sem=ls.at[dh - 1], recv_sem=lrs.at[dh - 1],
            device_id={"head": lax.rem(hd + dh, nh)}, device_id_type=MESH,
        )

    def step(u):
        dz = lax.rem(u // nx + 1, nz)
        dx = lax.rem(lax.rem(u, nx) + 1, nx)
        return dz, dx, lax.rem(z + dz, nz) * nx + lax.rem(x + dx, nx)

    def forward_sum(i, dz):
        for dx in range(1, nx):
            x_copy(i, dz, dx).wait_recv()
        s = lax.rem(z + dz, nz) * nx + x

        @pl.loop(0, outs[i].shape[0] // BLOCK)
        def _(r):
            at = pl.ds(pl.multiple_of(r * BLOCK, BLOCK), BLOCK)
            total = parts[i][s, at, :].astype(f32)
            for dx in range(1, nx):
                total += rx[i][dz, dx - 1, at, :].astype(f32)
            parts[i][s, at, :] = total.astype(bf16)

        z_copy(i, dz).start()

    def last_sum(i, factor):
        for dx in range(1, nx):
            x_copy(i, 0, dx).wait_recv()
        for dz in range(1, nz):
            z_copy(i, dz).wait_recv()

        @pl.loop(0, outs[i].shape[0] // BLOCK)
        def _(r):
            at = pl.ds(pl.multiple_of(r * BLOCK, BLOCK), BLOCK)
            total = parts[i][me, at, :].astype(f32)
            for dx in range(1, nx):
                total += rx[i][0, dx - 1, at, :].astype(f32)
            for dz in range(1, nz):
                total += rz[i][dz - 1, at, :].astype(f32)
            outs[i][at, :] = (total * factor).astype(bf16)

    share = dw_ref.shape[1]
    group = math.lcm(share, 128) // share

    def weight_part(p):
        span = group * share
        r = jnp.dot(
            ot_ref[...],
            grad_ref[:, pl.ds(pl.multiple_of(p * span, 128), span)],
            preferred_element_type=f32,
        ).astype(bf16)
        for t in range(group):
            wp[p * group + t] = r[:, t * share:(t + 1) * share]

    if group > 1:
        pl.loop(0, n_seq // group)(weight_part)

    @pl.loop(0, n_seq)
    def _(u):
        dz, dx, s = step(u)
        if group == 1:
            weight_part(s)

        @pl.when(dx > 0)
        def _():
            x_copy(0, dz, dx).start()

    lw = layer_ref.shape[1]

    @pl.loop(0, nh)
    def _(j):
        dh = lax.rem(j + 1, nh)
        at = pl.ds(pl.multiple_of(lax.rem(hd + dh, nh) * lw, 128), lw)
        lp[dh] = jnp.dot(o_ref[...], ow_ref[:, at], preferred_element_type=f32).astype(bf16)

        @pl.when(dh > 0)
        def _():
            l_copy(dh).start()

    acc[...] = jnp.zeros_like(acc)
    chunk = 640

    @pl.loop(0, grad_ref.shape[1] // chunk)
    def _(c):
        at = pl.ds(pl.multiple_of(c * chunk, 128), chunk)
        acc[...] += dot(grad_ref[:, at], ow_ref[:, at], 1, 1)

    g_ref[...] = acc[...].astype(bf16)
    acc[...] = jnp.zeros_like(acc)
    for h in range(heads):
        gt = g_ref[:, head(h)].astype(f32).T
        stat[h] = jnp.broadcast_to(
            jnp.sum(gt * ot_ref[head(h), :].astype(f32), axis=0, keepdims=True), (8, rows)
        )

    @pl.loop(0, n_seq)
    def _(u):
        dz, dx, s = step(u)
        for h in range(heads):
            q, g = q_ref[:, head(h)], g_ref[:, head(h)]
            k, v = k_ref[s, :, head(h)], v_ref[s, :, head(h)]
            w = jnp.exp2(scores(k, q, bias_ref[s]) - lse_ref[h, 0:1, :])
            vp[s, :, head(h)] = dot(w.astype(bf16), g, 1, 0).astype(bf16)
            ds = (w * (dot(v, g, 1, 1) - stat[h, 0:1, :])).astype(bf16)
            kp[s, :, head(h)] = dot(ds, q, 1, 0).astype(bf16)
            acc[head(h), :] += dot(k, ds, 0, 0)

        @pl.when(dx > 0)
        def _():
            x_copy(1, dz, dx).start()
            x_copy(2, dz, dx).start()

        @pl.when((dx == 0) & (dz > 0))
        def _():
            forward_sum(0, dz)

    dq_ref[...] = (acc[...] * scale).T.astype(bf16)

    @pl.loop(1, nz)
    def _(dz):
        forward_sum(1, dz)
        forward_sum(2, dz)

    @pl.loop(1, nh)
    def _(dh):
        l_copy(dh).wait_recv()

    @pl.loop(0, rows // BLOCK)
    def _(r):
        at = pl.ds(pl.multiple_of(r * BLOCK, BLOCK), BLOCK)
        total = lp[0, at, :].astype(f32)
        for dh in range(1, nh):
            total += lr[dh - 1, at, :].astype(f32)
        layer_ref[at, :] = total.astype(bf16)

    last_sum(0, 1.0)
    last_sum(1, scale)
    last_sum(2, 1.0)
    for i in range(3):
        for dz in range(nz):
            for dx in range(1, nx):
                x_copy(i, dz, dx).wait_send()
            if dz:
                z_copy(i, dz).wait_send()
    for dh in range(1, nh):
        l_copy(dh).wait_send()


def backward(n_seq, nh, queries, keys, values, attn, attn_t, lse, bias, full_grad, out_weight):
    nz, nx = NZ, n_seq // NZ
    rows, width = queries.shape
    columns = out_weight.shape[1]
    shapes = ((width, columns // n_seq), (rows, width), (rows, width))
    dma = pltpu.SemaphoreType.DMA
    x_sem, z_sem, l_sem = dma((3, nz, nx - 1)), dma((3, nz - 1)), dma((nh - 1,))
    one = jax.ShapeDtypeStruct((rows, width), bf16)
    return pl.pallas_call(
        functools.partial(backward_kernel, nz, nx, nh),
        out_shape=(
            jax.ShapeDtypeStruct((rows, columns // nh), bf16),
            one,
            one,
            one,
            jax.ShapeDtypeStruct(shapes[0], bf16),
        ),
        in_specs=[VMEM] * 9,
        out_specs=(VMEM,) * 5,
        scratch_shapes=[pltpu.VMEM((n_seq,) + s, bf16) for s in shapes]
        + [pltpu.VMEM((nz, nx - 1) + s, bf16) for s in shapes]
        + [pltpu.VMEM((nz - 1,) + s, bf16) for s in shapes]
        + [
            pltpu.VMEM((nh, rows, columns // nh), bf16),
            pltpu.VMEM((nh - 1, rows, columns // nh), bf16),
            pltpu.VMEM((rows, width), bf16),
            pltpu.VMEM((width, rows), f32),
            pltpu.VMEM((width // HD, 8, rows), f32),
        ]
        + [x_sem, x_sem, z_sem, z_sem, l_sem, l_sem],
        compiler_params=pltpu.CompilerParams(
            collective_id=1, has_side_effects=True, vmem_limit_bytes=60 * 2**20
        ),
    )(queries, keys, values, attn, attn_t, lse, bias, full_grad, out_weight)


def mask_bias(block_keys, key_count, frame_slot, seq_index, local_blocks):
    frames = frame_slot.shape[0]
    block_count, entries_count = block_keys.shape
    ids = jnp.arange(frames, dtype=jnp.int32)
    local_frames = local_blocks // PER_FRAME
    slots = seq_index * local_frames + jnp.arange(local_frames, dtype=jnp.int32)
    frame_at = jnp.sum(jnp.where(frame_slot[None, :] == slots[:, None], ids[None, :], 0), axis=1)
    logical = (frame_at[:, None] * PER_FRAME + jnp.arange(PER_FRAME)[None, :]).reshape(-1)
    all_blocks = jnp.arange(block_count, dtype=jnp.int32)
    pick = logical[:, None] == all_blocks[None, :]
    entries = jnp.sum(jnp.where(pick[:, :, None], block_keys[None], 0), axis=1)
    counts = jnp.sum(jnp.where(pick, key_count[None, :], 0), axis=1)
    slot_of = jnp.sum(
        jnp.where((entries // PER_FRAME)[..., None] == ids, frame_slot, 0), axis=-1
    )
    stored = slot_of * PER_FRAME + entries % PER_FRAME
    attended = jnp.arange(entries_count)[None, :] < counts[:, None]
    hit = jnp.any((stored[..., None] == all_blocks) & attended[..., None], axis=1)
    bias = jnp.where(hit, 0.0, NEG).astype(f32).T
    return jnp.repeat(bias, BLOCK, axis=1).reshape(frames, PER_FRAME, local_blocks * BLOCK)


def on_device(
    n_seq, n_head,
    queries, keys, values, out_weight, d_output, block_keys, key_count, frame_slot,
):
    rows, width = queries.shape
    seq_index = lax.axis_index("seq")
    bias = mask_bias(block_keys, key_count, frame_slot, seq_index, rows // BLOCK)
    full_grad = lax.all_gather(d_output, "head", axis=1, tiled=True)
    all_keys, all_values = gather_rows(keys, values, n_seq)
    attn, attn_t, lse = forward(queries, all_keys, all_values, bias)
    return store(
        backward(
            n_seq, n_head, queries, all_keys, all_values,
            attn, attn_t, lse, bias, full_grad, out_weight,
        )
    )


def solution(mesh):
    return jax.shard_map(
        functools.partial(on_device, mesh.shape["seq"], mesh.shape["head"]),
        mesh=mesh,
        in_specs=(
            P("seq", "head"),
            P("seq", "head"),
            P("seq", "head"),
            P("head", None),
            P("seq", "head"),
            P(),
            P(),
            P(),
        ),
        out_specs=(
            P("seq", "head"),
            P("seq", "head"),
            P("seq", "head"),
            P("seq", "head"),
            P("head", "seq"),
        ),
        check_vma=False,
    )
```
